1024 devices in a mesh: ka: 16 (over y, x), band: 32 (over z), grid: 2 (over core).
Axes of the slice: x: 4, y: 4, z: 32, core: 2. Of those that a mesh axis runs over, the one named last changes fastest.
Arguments:
- target_bands: float32 [16, 1, 2, 32, 1024], P('ka', None, None, 'grid'), may hold values from -6 to 6
- occupied: float32 [16, 32, 2, 32, 1024], P('ka', 'band', None, 'grid'), may hold values from -6 to 6
- qvectors: float32 [8, 3], replicated, may hold values from -1.5 to 1.5
- qmap: int32 [16], replicated, may hold values from 0 to 7
- cutoff: int32 [32, 1024], P('grid'), may hold values 0 or 1
Outputs:
- applied: float32 [16, 1, 2, 32, 1024], P('ka', None, None, 'grid')
The draws below stay inside these ranges and needn't reach their ends.
All inputs are finite; a program needn't handle non-finite values. No bound on the sum of `cutoff` on one device may be relied on, other than what follows from the above.
Results may differ from the reference program's by a relative error of at most 0.0003.
Values sent between devices are 32-bit elements; how exact they have to be, the bound alone decides.
A program may use at most 32 MiB of HBM per device.

```python
import math
import jax
import jax.numpy as jnp
from jax import lax

NX = 32
NY = 32
NZ = 32
NB = 1
NQ = 8
HOP = 1
K = 16
OCC = 32


def plant(drawn, rng, smallest, largest):
    longest = drawn.shape.index(max(drawn.shape))
    spots = []
    for shift in (0, 1):
        where = [jax.random.randint(jax.random.fold_in(rng, axis), (), 0, length) for axis, length in enumerate(drawn.shape)]
        where[longest] = (where[longest] + shift) % drawn.shape[longest]
        spots.append(tuple(where))
    return drawn.at[spots[0]].set(smallest).at[spots[1]].set(largest)


def level_of(rng, dims, split, low, high):
    def one(dim, shards_of):
        heights = jax.random.uniform(jax.random.fold_in(jax.random.fold_in(rng, 6), dim), (shards_of,), jnp.float32, low / len(split), high / len(split))
        return jnp.repeat(jnp.exp(heights), dims[dim] // shards_of).reshape((-1,) + (1,) * (len(dims) - dim - 1))

    factor_of = one(*split[0])
    for cut in split[1:]:
        factor_of = factor_of * one(*cut)
    return factor_of


def normal_values(own_key, dims, width, reach, cuts=(), kind=jnp.bfloat16):
    result = jax.random.normal(own_key, dims, jnp.float32) * width
    if len(cuts) > 0:
        result = level_of(own_key, dims, cuts, -0.22, 0.18) * result
    return jnp.clip(result, min=-reach, max=reach).astype(kind)


def setup_inputs(seed: int = 0) -> dict:
    arg_keys = jax.random.split(jax.random.key(seed), 6)
    return {
        "target_bands": normal_values(arg_keys[0], (K, NB, 2, NX, NY * NZ), 1.0, 6.0, ((0, 16), (3, 2)), jnp.float32),
        "occupied": normal_values(arg_keys[1], (K, OCC, 2, NX, NY * NZ), 1.0, 6.0, ((0, 16), (1, 32), (3, 2)), jnp.float32),
        "qvectors": jnp.clip(jax.random.uniform(arg_keys[2], (NQ, 3), jnp.float32, -1.5, 1.5), -1.5, 1.5),
        "qmap": plant(jax.random.randint(arg_keys[3], (K,), 0, NQ), jax.random.fold_in(arg_keys[3], 1), 0, NQ - 1).astype(jnp.int32),
        "cutoff": plant((jax.random.randint(arg_keys[4], (NX, NY * NZ), 0, 4) < 3).astype(jnp.int32), jax.random.fold_in(arg_keys[4], 1), 0, 1),
    }


SCREEN = 1.0
GSCALE = 0.5


def signed_freq(length):
    counter = jnp.arange(length, dtype=jnp.int32)
    return jnp.where(counter >= length // 2, counter - length, counter).astype(jnp.float32)


def kernel_full(qvector, cutoff):
    gx = signed_freq(NX) * GSCALE + qvector[0]
    gy = signed_freq(NY) * GSCALE + qvector[1]
    gz = signed_freq(NZ) * GSCALE + qvector[2]
    squares = gx[:, None, None] ** 2 + gy[None, :, None] ** 2 + gz[None, None, :] ** 2
    keep = cutoff.reshape(NX, NY, NZ).astype(jnp.float32)
    return 4.0 * math.pi * keep / (squares + SCREEN)


def apply_term(target, orbitals, kernel):
    nbands = target.shape[0]
    noccs = orbitals.shape[0]
    wave = lax.complex(target[:, 0], target[:, 1]).reshape(nbands, NX, NY, NZ)
    occ = lax.complex(orbitals[:, 0], orbitals[:, 1]).reshape(noccs, NX, NY, NZ)
    pair = jnp.conj(occ)[None] * wave[:, None]
    spectrum = jnp.fft.fftn(pair, axes=(2, 3, 4)) * kernel
    potential = jnp.fft.ifftn(spectrum, axes=(2, 3, 4))
    summed = jnp.sum(occ[None] * potential, axis=1).reshape(nbands, NX, NY * NZ)
    return jnp.stack([jnp.real(summed), jnp.imag(summed)], axis=1)


def reference(target_bands, occupied, qvectors, qmap, cutoff):
    count = target_bands.shape[0]
    kernel_zero = kernel_full(jnp.zeros((3,), jnp.float32), cutoff)

    def one_point(kpoint):
        partner = (kpoint + HOP) % count
        target = lax.dynamic_index_in_dim(target_bands, kpoint, 0, keepdims=False)
        own_occ = lax.dynamic_index_in_dim(occupied, kpoint, 0, keepdims=False)
        far_occ = lax.dynamic_index_in_dim(occupied, partner, 0, keepdims=False)
        qvector = qvectors[qmap[kpoint]]
        own_term = apply_term(target, own_occ, kernel_zero)
        far_term = apply_term(target, far_occ, kernel_full(qvector, cutoff))
        return -0.5 * (own_term + far_term)

    return lax.map(one_point, jnp.arange(count, dtype=jnp.int32))
```

```python
import functools
import math

import jax
import jax.numpy as jnp
import ml_dtypes
import numpy as np
from jax import lax
from jax.experimental import pallas as pl
from jax.experimental.pallas import tpu as pltpu
from jax.sharding import PartitionSpec as P

NX = 32
NY = 32
NZ = 32
HOP = 1
SCREEN = 1.0
GSCALE = 0.5

LANES = 128
BLOCKS = NY * NZ // LANES
HALF = NX // 2
GROUPS = 8
NEAR = (4, -4, 3, -3, 2, -2, 1, -1)
MESH = pl.DeviceIdType.MESH


def split_bf16(table):
    table = table.astype(np.float32)
    high = table.astype(ml_dtypes.bfloat16)
    low = (table - high.astype(np.float32)).astype(ml_dtypes.bfloat16)
    return high, low


def make_tables():
    lane = np.arange(LANES)
    low_y, z = lane // NZ, lane % NZ
    phase = np.outer(low_y, low_y) / 4.0 + (np.outer(z, z) % NZ) / NZ
    cos, sin = np.cos(2 * np.pi * phase), np.sin(2 * np.pi * phase)
    forward = np.block([[cos, -sin], [sin, cos]])
    backward = np.block([[cos, sin], [-sin, cos]])
    yz = np.stack([*split_bf16(forward), *split_bf16(backward)])
    x = np.arange(NX)
    angle = 2 * np.pi * (np.outer(x, x) % NX) / NX
    cos, sin = np.cos(angle), np.sin(angle)
    rows = []
    for mat in (np.block([[cos, sin], [-sin, cos]]), np.block([[cos, -sin], [sin, cos]])):
        high, low = split_bf16(mat)
        rows.append(np.concatenate([high, low, high], axis=1))
    turn = 2 * np.pi * np.outer(np.arange(BLOCKS), low_y) / NY
    twiddle = np.concatenate([np.cos(turn), -np.sin(turn)]).astype(np.float32)
    return yz, np.stack(rows), twiddle


def butterflies(real, imag, sign):
    count = len(real)
    if count == 1:
        return real, imag
    even_r, even_i = butterflies(real[::2], imag[::2], sign)
    odd_r, odd_i = butterflies(real[1::2], imag[1::2], sign)
    half = count // 2
    root = math.sqrt(0.5)
    out_r, out_i = [None] * count, [None] * count
    for k in range(half):
        r, i = odd_r[k], odd_i[k]
        turn = k * 8 // count
        if turn == 1:
            r, i = ((r - i) * root, (i + r) * root) if sign > 0 else ((r + i) * root, (i - r) * root)
        elif turn == 2:
            r, i = (-i, r) if sign > 0 else (i, -r)
        elif turn == 3:
            r, i = ((-r - i) * root, (r - i) * root) if sign > 0 else ((i - r) * root, (-i - r) * root)
        out_r[k], out_i[k] = even_r[k] + r, even_i[k] + i
        out_r[k + half], out_i[k + half] = even_r[k] - r, even_i[k] - i
    return out_r, out_i


def halves(value):
    high = value.astype(jnp.bfloat16)
    return high, (value - high.astype(jnp.float32)).astype(jnp.bfloat16)


def mul(a, b):
    return jnp.dot(a, b, preferred_element_type=jnp.float32)


def yz_product(real, imag, high_tab, low_tab):
    rows = jnp.concatenate(
        [jnp.concatenate(real, axis=0), jnp.concatenate(imag, axis=0)], axis=1
    )
    high, low = halves(rows)
    out = mul(high, high_tab) + (mul(low, high_tab) + mul(high, low_tab))
    real = [out[NX * b : NX * (b + 1), :LANES] for b in range(BLOCKS)]
    imag = [out[NX * b : NX * (b + 1), LANES:] for b in range(BLOCKS)]
    return real, imag


def x_product(cols, tab):
    high, low = halves(cols)
    return mul(tab, jnp.concatenate([high, high, low], axis=0))


def pair_potential(rho_r, rho_i, kernel, yz_tab, x_tab, tw_r, tw_i):
    real, imag = butterflies(rho_r, rho_i, -1)
    turned_r = [real[c] * tw_r[c] - imag[c] * tw_i[c] for c in range(BLOCKS)]
    turned_i = [real[c] * tw_i[c] + imag[c] * tw_r[c] for c in range(BLOCKS)]
    real, imag = yz_product(turned_r, turned_i, yz_tab[0], yz_tab[1])
    cols = jnp.concatenate(
        [jnp.concatenate([real[c], imag[c]], axis=0) for c in range(BLOCKS)], axis=1
    )
    spectrum = x_product(cols, x_tab[0])
    weight = jnp.concatenate(kernel, axis=1)
    spectrum = spectrum * jnp.concatenate([weight, weight], axis=0)
    cols = x_product(spectrum, x_tab[1])
    real = [cols[:NX, LANES * c : LANES * (c + 1)] for c in range(BLOCKS)]
    imag = [cols[NX:, LANES * c : LANES * (c + 1)] for c in range(BLOCKS)]
    real, imag = yz_product(real, imag, yz_tab[2], yz_tab[3])
    turned_r = [real[c] * tw_r[c] + imag[c] * tw_i[c] for c in range(BLOCKS)]
    turned_i = [imag[c] * tw_r[c] - real[c] * tw_i[c] for c in range(BLOCKS)]
    return butterflies(turned_r, turned_i, 1)


def signed(index, length):
    return jnp.where(index >= length // 2, index - length, index).astype(jnp.float32)


def screened(block, qx, qy, qz):
    shape = (NX, LANES)
    lane = lax.broadcasted_iota(jnp.int32, shape, 1)
    gx = signed(lax.broadcasted_iota(jnp.int32, shape, 0), NX) * GSCALE + qx
    gy = signed(block + 8 * (lane // NZ), NY) * GSCALE + qy
    gz = signed(lane % NZ, NZ) * GSCALE + qz
    squares = gx * gx + gy * gy + gz * gz
    return (4.0 * math.pi * -0.5 / (NX * NY * NZ)) / (squares + SCREEN)


def reordered(keep, block, roll):
    group = lax.broadcasted_iota(jnp.int32, (NX, LANES), 1) // NZ
    out = None
    for d in range(4):
        source, place = 2 * d + block // 4, block % 4
        piece = roll(keep(source), ((d - place) * NZ) % LANES)
        out = piece if out is None else jnp.where(group == d, piece, out)
    return out


def kernel(
    tgt_in, occ_in, qvectors, qmap, cut_in, yz_tab, x_tab, twiddle,
    out_ref,
    tgt, occ, cut, weight, part, other, summed, near, own, mid, far, total, gathered,
    local_sem, occ_recv, in_send, in_recv, near_send, near_recv, mid_send, mid_recv, back_send, back_recv,
):
    k = lax.axis_index("ka")
    z = lax.axis_index("band")
    core = lax.axis_index("grid")
    far_core = 1 - core
    points = lax.axis_size("ka")
    chips = lax.axis_size("band")

    def chip(delta):
        return lax.rem(z + delta + chips, chips)

    def remote(src, dst, send, recv, where):
        return pltpu.make_async_remote_copy(
            src_ref=src, dst_ref=dst, send_sem=send, recv_sem=recv, device_id=where, device_id_type=MESH
        )

    locals_ = [
        pltpu.make_async_copy(tgt_in.at[0, 0], tgt.at[core], local_sem.at[0]),
        pltpu.make_async_copy(cut_in, cut.at[core], local_sem.at[1]),
    ]
    for copy in locals_:
        copy.start()
    own_occ = pltpu.make_async_copy(occ_in.at[0, 0], occ.at[0], local_sem.at[2])

    @pl.when(core == 0)
    def _():
        own_occ.start()

    barrier = pltpu.get_barrier_semaphore()
    pl.semaphore_signal(barrier, inc=1, device_id={"grid": far_core}, device_id_type=MESH)

    @pl.when(core == 1)
    def _():
        source = lax.rem(k + HOP, points)
        for c in range(2):
            pl.semaphore_signal(barrier, inc=1, device_id={"ka": source, "grid": c}, device_id_type=MESH)

    for delta in NEAR:
        pl.semaphore_signal(barrier, inc=1, device_id={"band": chip(delta)}, device_id_type=MESH)
    pl.semaphore_wait(barrier, 2 + len(NEAR))

    user = lax.rem(k - HOP + points, points)
    sent = [
        remote(occ_in.at[0, 0], occ.at[core], in_send.at[0], occ_recv.at[core], {"ka": user, "grid": 1}),
        remote(tgt_in.at[0, 0], tgt.at[core], in_send.at[1], in_recv.at[1], {"grid": far_core}),
        remote(cut_in, cut.at[core], in_send.at[2], in_recv.at[2], {"grid": far_core}),
    ]
    for copy in sent:
        copy.start()
    cross = remote(occ_in.at[0, 0], occ.at[1], in_send.at[3], occ_recv.at[1], {"grid": 0})

    @pl.when(core == 1)
    def _():
        cross.start()

    chosen = qmap[k]
    used = core.astype(jnp.float32)
    qx, qy, qz = (qvectors[chosen, d] * used for d in range(3))
    for block in range(BLOCKS):
        weight[block] = screened(block, qx, qy, qz)

    locals_[1].wait()
    sent[2].wait_recv()

    def keep(block):
        lanes = slice(LANES * block, LANES * (block + 1))
        return jnp.concatenate([cut[0, :, lanes], cut[1, :, lanes]], axis=0).astype(jnp.float32)

    for block in range(BLOCKS):
        weight[block] = weight[block] * reordered(keep, block, lambda v, s: pltpu.roll(v, s, 1))

    locals_[0].wait()
    sent[1].wait_recv()

    @pl.when(core == 0)
    def _():
        own_occ.wait()
        cross.wait_recv()

    @pl.when(core == 1)
    def _():
        for c in range(2):
            remote(occ_in.at[0, 0], occ.at[c], in_send.at[0], occ_recv.at[c], {"grid": 0}).wait_recv()

    def block_of(ref, which, block):
        lanes = slice(LANES * block, LANES * (block + 1))
        return jnp.concatenate([ref[0, which, :, lanes], ref[1, which, :, lanes]], axis=0)

    rho_r, rho_i = [], []
    for block in range(BLOCKS):
        t_r, t_i = block_of(tgt, 0, block), block_of(tgt, 1, block)
        o_r, o_i = block_of(occ, 0, block), block_of(occ, 1, block)
        rho_r.append(o_r * t_r + o_i * t_i)
        rho_i.append(o_r * t_i - o_i * t_r)
    pot_r, pot_i = pair_potential(
        rho_r,
        rho_i,
        [weight[block] for block in range(BLOCKS)],
        [yz_tab[i] for i in range(4)],
        [x_tab[i] for i in range(2)],
        [twiddle[c : c + 1, :] for c in range(BLOCKS)],
        [twiddle[BLOCKS + c : BLOCKS + c + 1, :] for c in range(BLOCKS)],
    )
    for block in range(BLOCKS):
        o_r, o_i = block_of(occ, 0, block), block_of(occ, 1, block)
        app_r = o_r * pot_r[block] - o_i * pot_i[block]
        app_i = o_r * pot_i[block] + o_i * pot_r[block]
        for half in range(2):
            rows = slice(HALF * half, HALF * (half + 1))
            part[half, block, 0] = app_r[rows]
            part[half, block, 1] = app_i[rows]

    crossing = remote(part.at[far_core], other, in_send.at[4], in_recv.at[4], {"grid": far_core})
    crossing.start()
    crossing.wait_recv()
    summed[...] = part[core] + other[...]

    group = lax.rem(z, GROUPS)

    def pieces(ref, index, delta):
        if abs(delta) < 4:
            return ref.at[index]
        return ref.at[index, 0 if delta > 0 else 1]

    copies = []
    for n, delta in enumerate(NEAR):
        theirs = lax.rem(z + delta + GROUPS, GROUPS)
        slot = 0 if abs(delta) == 4 else n - 1
        copies.append(
            remote(
                pieces(summed, theirs, delta),
                pieces(near, slot, delta),
                near_send.at[n],
                near_recv.at[n],
                {"band": chip(delta)},
            )
        )
        copies[-1].start()
    value = summed[group]
    for copy in copies[::-1]:
        copy.wait_recv()
    for slot in range(len(NEAR) - 1):
        value = value + near[slot]
    own[...] = value

    first = [
        remote(own, mid.at[n], mid_send.at[n], mid_recv.at[n], {"band": chip(delta)})
        for n, delta in enumerate((8, -8))
    ]
    for copy in first:
        copy.start()
    second = [
        remote(mid.at[n, n], far.at[n], mid_send.at[2 + n], mid_recv.at[2 + n], {"band": chip(delta)})
        for n, delta in enumerate((8, -8))
    ]
    for n in range(2):
        first[n].wait_recv()
        second[n].start()
    for copy in second:
        copy.wait_recv()
    value = (own[...] + far[...]) + (mid[0] + mid[1])
    total[...] = value
    gathered[group] = value

    back = []
    for n, delta in enumerate(NEAR):
        source = total if abs(delta) < 4 else total.at[0 if delta > 0 else 1]
        back.append(
            remote(
                source, pieces(gathered, group, delta), back_send.at[n], back_recv.at[n], {"band": chip(delta)}
            )
        )
        back[-1].start()
    for copy in back[::-1]:
        copy.wait_recv()
    for block in range(BLOCKS):
        lanes = slice(LANES * block, LANES * (block + 1))
        for which in range(2):
            out_ref[0, 0, which, :, lanes] = gathered[block, which]

    for copy in [*sent, crossing, *copies, *first, *second, *back]:
        copy.wait_send()

    @pl.when(core == 1)
    def _():
        cross.wait_send()


def shards(target_bands, occupied, qvectors, qmap, cutoff):
    yz_tab, x_tab, twiddle = make_tables()
    f32 = jnp.float32
    planes = (2, HALF, NY * NZ)
    tile = (2, HALF, LANES)
    dma = pltpu.SemaphoreType.DMA
    vmem = pl.BlockSpec(memory_space=pltpu.VMEM)
    smem = pl.BlockSpec(memory_space=pltpu.SMEM)
    anywhere = pl.BlockSpec(memory_space=pl.ANY)
    return pl.pallas_call(
        kernel,
        out_shape=jax.ShapeDtypeStruct(target_bands.shape, f32),
        in_specs=[anywhere, anywhere, smem, smem, anywhere, vmem, vmem, vmem],
        out_specs=vmem,
        scratch_shapes=[
            pltpu.VMEM((2,) + planes, f32),
            pltpu.VMEM((2,) + planes, f32),
            pltpu.VMEM(planes, jnp.int32),
            pltpu.VMEM((BLOCKS, NX, LANES), f32),
            pltpu.VMEM((2, BLOCKS) + tile, f32),
            pltpu.VMEM((BLOCKS,) + tile, f32),
            pltpu.VMEM((BLOCKS,) + tile, f32),
            pltpu.VMEM((len(NEAR) - 1,) + tile, f32),
            pltpu.VMEM(tile, f32),
            pltpu.VMEM((2,) + tile, f32),
            pltpu.VMEM(tile, f32),
            pltpu.VMEM(tile, f32),
            pltpu.VMEM((GROUPS,) + tile, f32),
            dma((3,)),
            dma((2,)),
            dma((5,)),
            dma((5,)),
            dma((len(NEAR),)),
            dma((len(NEAR),)),
            dma((4,)),
            dma((4,)),
            dma((len(NEAR),)),
            dma((len(NEAR),)),
        ],
        compiler_params=pltpu.CompilerParams(collective_id=0, has_side_effects=True),
    )(
        target_bands,
        occupied,
        qvectors,
        qmap,
        cutoff,
        jnp.asarray(yz_tab),
        jnp.asarray(x_tab),
        jnp.asarray(twiddle),
    )


def solution(mesh):
    return jax.shard_map(
        shards,
        mesh=mesh,
        in_specs=(
            P("ka", None, None, "grid", None),
            P("ka", "band", None, "grid", None),
            P(),
            P(),
            P("grid", None),
        ),
        out_specs=P("ka", None, None, "grid", None),
        check_vma=False,
    )
```

```python
import functools
import math

import jax
import jax.numpy as jnp
import ml_dtypes
import numpy as np
from jax import lax
from jax.experimental import pallas as pl
from jax.experimental.pallas import tpu as pltpu
from jax.sharding import PartitionSpec as P

NX = 32
NY = 32
NZ = 32
HOP = 1
SCREEN = 1.0
GSCALE = 0.5

LANES = 128
BLOCKS = NY * NZ // LANES
HALF = NX // 2
GROUPS = 8
NEAR = (4, -4, 3, -3, 2, -2, 1, -1)
MESH = pl.DeviceIdType.MESH


def split_bf16(table):
    table = table.astype(np.float32)
    high = table.astype(ml_dtypes.bfloat16)
    low = (table - high.astype(np.float32)).astype(ml_dtypes.bfloat16)
    return high, low


def make_tables():
    lane = np.arange(LANES)
    low_y, z = lane // NZ, lane % NZ
    phase = np.outer(low_y, low_y) / 4.0 + (np.outer(z, z) % NZ) / NZ
    cos, sin = np.cos(2 * np.pi * phase), np.sin(2 * np.pi * phase)
    forward = np.block([[cos, -sin], [sin, cos]])
    backward = np.block([[cos, sin], [-sin, cos]])
    yz = np.stack([*split_bf16(forward), *split_bf16(backward)])
    x = np.arange(NX)
    angle = 2 * np.pi * (np.outer(x, x) % NX) / NX
    cos, sin = np.cos(angle), np.sin(angle)
    rows = []
    for mat in (np.block([[cos, sin], [-sin, cos]]), np.block([[cos, -sin], [sin, cos]])):
        high, low = split_bf16(mat)
        rows.append(np.concatenate([high, low, high], axis=1))
    turn = 2 * np.pi * np.outer(np.arange(BLOCKS), low_y) / NY
    twiddle = np.concatenate([np.cos(turn), -np.sin(turn)]).astype(np.float32)
    return yz, np.stack(rows), twiddle


def butterflies(real, imag, sign):
    count = len(real)
    if count == 1:
        return real, imag
    even_r, even_i = butterflies(real[::2], imag[::2], sign)
    odd_r, odd_i = butterflies(real[1::2], imag[1::2], sign)
    half = count // 2
    root = math.sqrt(0.5)
    out_r, out_i = [None] * count, [None] * count
    for k in range(half):
        r, i = odd_r[k], odd_i[k]
        turn = k * 8 // count
        if turn == 1:
            r, i = ((r - i) * root, (i + r) * root) if sign > 0 else ((r + i) * root, (i - r) * root)
        elif turn == 2:
            r, i = (-i, r) if sign > 0 else (i, -r)
        elif turn == 3:
            r, i = ((-r - i) * root, (r - i) * root) if sign > 0 else ((i - r) * root, (-i - r) * root)
        out_r[k], out_i[k] = even_r[k] + r, even_i[k] + i
        out_r[k + half], out_i[k + half] = even_r[k] - r, even_i[k] - i
    return out_r, out_i


def halves(value):
    high = value.astype(jnp.bfloat16)
    return high, (value - high.astype(jnp.float32)).astype(jnp.bfloat16)


def mul(a, b):
    return jnp.dot(a, b, preferred_element_type=jnp.float32)


def yz_product(real, imag, high_tab, low_tab):
    rows = jnp.concatenate(
        [jnp.concatenate(real, axis=0), jnp.concatenate(imag, axis=0)], axis=1
    )
    high, low = halves(rows)
    out = mul(high, high_tab) + (mul(low, high_tab) + mul(high, low_tab))
    real = [out[NX * b : NX * (b + 1), :LANES] for b in range(BLOCKS)]
    imag = [out[NX * b : NX * (b + 1), LANES:] for b in range(BLOCKS)]
    return real, imag


def x_product(cols, tab):
    high, low = halves(cols)
    return mul(tab, jnp.concatenate([high, high, low], axis=0))


def pair_potential(rho_r, rho_i, kernel, yz_tab, x_tab, tw_r, tw_i):
    real, imag = butterflies(rho_r, rho_i, -1)
    turned_r = [real[c] * tw_r[c] - imag[c] * tw_i[c] for c in range(BLOCKS)]
    turned_i = [real[c] * tw_i[c] + imag[c] * tw_r[c] for c in range(BLOCKS)]
    real, imag = yz_product(turned_r, turned_i, yz_tab[0], yz_tab[1])
    cols = jnp.concatenate(
        [jnp.concatenate([real[c], imag[c]], axis=0) for c in range(BLOCKS)], axis=1
    )
    spectrum = x_product(cols, x_tab[0])
    weight = jnp.concatenate(kernel, axis=1)
    spectrum = spectrum * jnp.concatenate([weight, weight], axis=0)
    cols = x_product(spectrum, x_tab[1])
    real = [cols[:NX, LANES * c : LANES * (c + 1)] for c in range(BLOCKS)]
    imag = [cols[NX:, LANES * c : LANES * (c + 1)] for c in range(BLOCKS)]
    real, imag = yz_product(real, imag, yz_tab[2], yz_tab[3])
    turned_r = [real[c] * tw_r[c] + imag[c] * tw_i[c] for c in range(BLOCKS)]
    turned_i = [imag[c] * tw_r[c] - real[c] * tw_i[c] for c in range(BLOCKS)]
    return butterflies(turned_r, turned_i, 1)


def signed(index, length):
    return jnp.where(index >= length // 2, index - length, index).astype(jnp.float32)


def screened(block, qx, qy, qz):
    shape = (NX, LANES)
    lane = lax.broadcasted_iota(jnp.int32, shape, 1)
    gx = signed(lax.broadcasted_iota(jnp.int32, shape, 0), NX) * GSCALE + qx
    gy = signed(block + 8 * (lane // NZ), NY) * GSCALE + qy
    gz = signed(lane % NZ, NZ) * GSCALE + qz
    squares = gx * gx + gy * gy + gz * gz
    return (4.0 * math.pi * -0.5 / (NX * NY * NZ)) / (squares + SCREEN)


def reordered(keep, block, roll):
    group = lax.broadcasted_iota(jnp.int32, (NX, LANES), 1) // NZ
    out = None
    for d in range(4):
        source, place = 2 * d + block // 4, block % 4
        piece = roll(keep(source), ((d - place) * NZ) % LANES)
        out = piece if out is None else jnp.where(group == d, piece, out)
    return out


def kernel(
    tgt_in, occ_in, qvectors, qmap, cut_in, yz_in, x_in, twiddle_in,
    out_ref,
    yz_tab, x_tab, twiddle, tgt, occ, cut, weight, part, other, summed, near, own, mid, total, gathered,
    entered, local_sem, occ_recv, in_send, in_recv, near_send, near_recv, mid_send, mid_recv, back_send, back_recv,
):
    k = lax.axis_index("ka")
    z = lax.axis_index("band")
    core = lax.axis_index("grid")
    far_core = 1 - core
    points = lax.axis_size("ka")
    chips = lax.axis_size("band")

    def chip(delta):
        return lax.rem(z + delta + chips, chips)

    def remote(src, dst, send, recv, where):
        return pltpu.make_async_remote_copy(
            src_ref=src, dst_ref=dst, send_sem=send, recv_sem=recv, device_id=where, device_id_type=MESH
        )

    locals_ = [
        pltpu.make_async_copy(tgt_in.at[0, 0], tgt.at[core], local_sem.at[0]),
        pltpu.make_async_copy(cut_in, cut.at[core], local_sem.at[1]),
        pltpu.make_async_copy(yz_in, yz_tab, local_sem.at[3]),
        pltpu.make_async_copy(x_in, x_tab, local_sem.at[4]),
        pltpu.make_async_copy(twiddle_in, twiddle, local_sem.at[5]),
    ]
    barrier = pltpu.get_barrier_semaphore()
    pl.semaphore_signal(barrier, inc=1, device_id={"grid": far_core}, device_id_type=MESH)

    @pl.when(core == 1)
    def _():
        source = lax.rem(k + HOP, points)
        for c in range(2):
            pl.semaphore_signal(barrier, inc=1, device_id={"ka": source, "grid": c}, device_id_type=MESH)

    for delta in NEAR:
        pl.semaphore_signal(barrier, inc=1, device_id={"band": chip(delta)}, device_id_type=MESH)

    for copy in locals_:
        copy.start()
    own_occ = pltpu.make_async_copy(occ_in.at[0, 0], occ.at[0], local_sem.at[2])

    @pl.when(core == 0)
    def _():
        own_occ.start()

    pl.semaphore_wait(barrier, 2 + len(NEAR))

    def tell(stage):
        for delta in (4, -4):
            pl.semaphore_signal(entered.at[stage], inc=1, device_id={"band": chip(delta)}, device_id_type=MESH)

    def hear(stage):
        pl.semaphore_wait(entered.at[stage], 2)

    user = lax.rem(k - HOP + points, points)
    sent = [
        remote(occ_in.at[0, 0], occ.at[core], in_send.at[0], occ_recv.at[core], {"ka": user, "grid": 1}),
        remote(tgt_in.at[0, 0], tgt.at[core], in_send.at[1], in_recv.at[1], {"grid": far_core}),
        remote(cut_in, cut.at[core], in_send.at[2], in_recv.at[2], {"grid": far_core}),
    ]
    for copy in sent:
        copy.start()
    cross = remote(occ_in.at[0, 0], occ.at[1], in_send.at[3], occ_recv.at[1], {"grid": 0})

    @pl.when(core == 1)
    def _():
        cross.start()

    tell(0)
    chosen = qmap[k]
    used = core.astype(jnp.float32)
    qx, qy, qz = (qvectors[d, chosen] * used for d in range(3))
    for block in range(BLOCKS):
        weight[block] = screened(block, qx, qy, qz)

    locals_[1].wait()
    sent[2].wait_recv()

    def keep(block):
        lanes = slice(LANES * block, LANES * (block + 1))
        return jnp.concatenate([cut[0, :, lanes], cut[1, :, lanes]], axis=0).astype(jnp.float32)

    for block in range(BLOCKS):
        weight[block] = weight[block] * reordered(keep, block, lambda v, s: pltpu.roll(v, s, 1))

    for n in (0, 2, 3, 4):
        locals_[n].wait()
    sent[1].wait_recv()
    hear(0)
    tell(1)

    @pl.when(core == 0)
    def _():
        own_occ.wait()
        cross.wait_recv()

    @pl.when(core == 1)
    def _():
        for c in range(2):
            remote(occ_in.at[0, 0], occ.at[c], in_send.at[0], occ_recv.at[c], {"grid": 0}).wait_recv()

    def block_of(ref, which, block):
        lanes = slice(LANES * block, LANES * (block + 1))
        return jnp.concatenate([ref[0, which, :, lanes], ref[1, which, :, lanes]], axis=0)

    rho_r, rho_i = [], []
    for block in range(BLOCKS):
        t_r, t_i = block_of(tgt, 0, block), block_of(tgt, 1, block)
        o_r, o_i = block_of(occ, 0, block), block_of(occ, 1, block)
        rho_r.append(o_r * t_r + o_i * t_i)
        rho_i.append(o_r * t_i - o_i * t_r)
    pot_r, pot_i = pair_potential(
        rho_r,
        rho_i,
        [weight[block] for block in range(BLOCKS)],
        [yz_tab[i] for i in range(4)],
        [x_tab[i] for i in range(2)],
        [twiddle[c : c + 1, :] for c in range(BLOCKS)],
        [twiddle[BLOCKS + c : BLOCKS + c + 1, :] for c in range(BLOCKS)],
    )
    for block in range(BLOCKS):
        o_r, o_i = block_of(occ, 0, block), block_of(occ, 1, block)
        app_r = o_r * pot_r[block] - o_i * pot_i[block]
        app_i = o_r * pot_i[block] + o_i * pot_r[block]
        for half in range(2):
            rows = slice(HALF * half, HALF * (half + 1))
            part[half, block, 0] = app_r[rows]
            part[half, block, 1] = app_i[rows]

    crossing = remote(part.at[far_core], other, in_send.at[4], in_recv.at[4], {"grid": far_core})
    crossing.start()
    crossing.wait_recv()
    summed[...] = part[core] + other[...]

    group = lax.rem(z, GROUPS)

    def pieces(ref, index, delta):
        if abs(delta) < 4:
            return ref.at[index]
        return ref.at[index, 0 if delta > 0 else 1]

    copies = []
    for n, delta in enumerate(NEAR):
        theirs = lax.rem(z + delta + GROUPS, GROUPS)
        slot = 0 if abs(delta) == 4 else n - 1
        copies.append(
            remote(
                pieces(summed, theirs, delta),
                pieces(near, slot, delta),
                near_send.at[n],
                near_recv.at[n],
                {"band": chip(delta)},
            )
        )
        copies[-1].start()
    value = summed[group]
    for copy in copies[::-1]:
        copy.wait_recv()
    for slot in range(len(NEAR) - 1):
        value = value + near[slot]
    own[...] = value

    hear(1)
    across = [
        remote(own, mid.at[n], mid_send.at[n], mid_recv.at[n], {"band": chip(delta)})
        for n, delta in enumerate((12, -12, 4, -4))
    ]
    for copy in across:
        copy.start()
    for copy in across[::-1]:
        copy.wait_recv()
    value = (mid[0] + mid[3]) + (mid[1] + mid[2])
    group = lax.rem(z + 4, GROUPS)
    total[...] = value
    gathered[group] = value

    back = []
    for n, delta in enumerate(NEAR):
        source = total if abs(delta) < 4 else total.at[0 if delta > 0 else 1]
        back.append(
            remote(
                source, pieces(gathered, group, delta), back_send.at[n], back_recv.at[n], {"band": chip(delta)}
            )
        )
        back[-1].start()
    for copy in back[::-1]:
        copy.wait_recv()
    for block in range(BLOCKS):
        lanes = slice(LANES * block, LANES * (block + 1))
        for which in range(2):
            out_ref[0, 0, which, :, lanes] = gathered[block, which]

    for copy in [*sent, crossing, *copies, *across, *back]:
        copy.wait_send()

    @pl.when(core == 1)
    def _():
        cross.wait_send()


def shards(target_bands, occupied, qvectors, qmap, cutoff):
    yz_tab, x_tab, twiddle = make_tables()
    f32 = jnp.float32
    planes = (2, HALF, NY * NZ)
    tile = (2, HALF, LANES)
    dma = pltpu.SemaphoreType.DMA
    vmem = pl.BlockSpec(memory_space=pltpu.VMEM)
    smem = pl.BlockSpec(memory_space=pltpu.SMEM)
    anywhere = pl.BlockSpec(memory_space=pl.ANY)
    return pl.pallas_call(
        kernel,
        out_shape=jax.ShapeDtypeStruct(target_bands.shape, f32),
        in_specs=[anywhere, anywhere, smem, smem] + [anywhere] * 4,
        out_specs=vmem,
        scratch_shapes=[
            pltpu.VMEM(yz_tab.shape, jnp.bfloat16),
            pltpu.VMEM(x_tab.shape, jnp.bfloat16),
            pltpu.VMEM(twiddle.shape, f32),
            pltpu.VMEM((2,) + planes, f32),
            pltpu.VMEM((2,) + planes, f32),
            pltpu.VMEM(planes, jnp.int32),
            pltpu.VMEM((BLOCKS, NX, LANES), f32),
            pltpu.VMEM((2, BLOCKS) + tile, f32),
            pltpu.VMEM((BLOCKS,) + tile, f32),
            pltpu.VMEM((BLOCKS,) + tile, f32),
            pltpu.VMEM((len(NEAR) - 1,) + tile, f32),
            pltpu.VMEM(tile, f32),
            pltpu.VMEM((4,) + tile, f32),
            pltpu.VMEM(tile, f32),
            pltpu.VMEM((GROUPS,) + tile, f32),
            pltpu.SemaphoreType.REGULAR((2,)),
            dma((6,)),
            dma((2,)),
            dma((5,)),
            dma((5,)),
            dma((len(NEAR),)),
            dma((len(NEAR),)),
            dma((4,)),
            dma((4,)),
            dma((len(NEAR),)),
            dma((len(NEAR),)),
        ],
        compiler_params=pltpu.CompilerParams(collective_id=0, has_side_effects=True),
    )(
        target_bands,
        occupied,
        qvectors.T,
        qmap,
        cutoff,
        jnp.asarray(yz_tab),
        jnp.asarray(x_tab),
        jnp.asarray(twiddle),
    )


def solution(mesh):
    return jax.shard_map(
        shards,
        mesh=mesh,
        in_specs=(
            P("ka", None, None, "grid", None),
            P("ka", "band", None, "grid", None),
            P(),
            P(),
            P("grid", None),
        ),
        out_specs=P("ka", None, None, "grid", None),
        check_vma=False,
    )
```

```python
import functools
import math

import jax
import jax.numpy as jnp
import ml_dtypes
import numpy as np
from jax import lax
from jax.experimental import pallas as pl
from jax.experimental.pallas import tpu as pltpu
from jax.sharding import PartitionSpec as P

NX = 32
NY = 32
NZ = 32
HOP = 1
SCREEN = 1.0
GSCALE = 0.5

LANES = 128
BLOCKS = NY * NZ // LANES
HALF = NX // 2
GROUPS = 8
NEAR = (4, -4, 3, -3, 2, -2, 1, -1)
MESH = pl.DeviceIdType.MESH


def split_bf16(table):
    table = table.astype(np.float32)
    high = table.astype(ml_dtypes.bfloat16)
    low = (table - high.astype(np.float32)).astype(ml_dtypes.bfloat16)
    return high, low


def make_tables():
    lane = np.arange(LANES)
    low_y, z = lane // NZ, lane % NZ
    phase = np.outer(low_y, low_y) / 4.0 + (np.outer(z, z) % NZ) / NZ
    cos, sin = np.cos(2 * np.pi * phase), np.sin(2 * np.pi * phase)
    forward = np.block([[cos, -sin], [sin, cos]])
    backward = np.block([[cos, sin], [-sin, cos]])
    yz = np.stack([*split_bf16(forward), *split_bf16(backward)])
    x = np.arange(NX)
    angle = 2 * np.pi * (np.outer(x, x) % NX) / NX
    cos, sin = np.cos(angle), np.sin(angle)
    rows = []
    for mat in (np.block([[cos, sin], [-sin, cos]]), np.block([[cos, -sin], [sin, cos]])):
        high, low = split_bf16(mat)
        rows.append(np.concatenate([high, low, high], axis=1))
    turn = 2 * np.pi * np.outer(np.arange(BLOCKS), low_y) / NY
    twiddle = np.concatenate([np.cos(turn), -np.sin(turn)]).astype(np.float32)
    return yz, np.stack(rows), twiddle


def butterflies(real, imag, sign):
    count = len(real)
    if count == 1:
        return real, imag
    even_r, even_i = butterflies(real[::2], imag[::2], sign)
    odd_r, odd_i = butterflies(real[1::2], imag[1::2], sign)
    half = count // 2
    root = math.sqrt(0.5)
    out_r, out_i = [None] * count, [None] * count
    for k in range(half):
        r, i = odd_r[k], odd_i[k]
        turn = k * 8 // count
        if turn == 1:
            r, i = ((r - i) * root, (i + r) * root) if sign > 0 else ((r + i) * root, (i - r) * root)
        elif turn == 2:
            r, i = (-i, r) if sign > 0 else (i, -r)
        elif turn == 3:
            r, i = ((-r - i) * root, (r - i) * root) if sign > 0 else ((i - r) * root, (-i - r) * root)
        out_r[k], out_i[k] = even_r[k] + r, even_i[k] + i
        out_r[k + half], out_i[k + half] = even_r[k] - r, even_i[k] - i
    return out_r, out_i


def halves(value):
    high = value.astype(jnp.bfloat16)
    return high, (value - high.astype(jnp.float32)).astype(jnp.bfloat16)


def mul(a, b):
    return jnp.dot(a, b, preferred_element_type=jnp.float32)


def yz_product(real, imag, high_tab, low_tab):
    rows = jnp.concatenate(
        [jnp.concatenate(real, axis=0), jnp.concatenate(imag, axis=0)], axis=1
    )
    high, low = halves(rows)
    out = mul(high, high_tab) + (mul(low, high_tab) + mul(high, low_tab))
    real = [out[NX * b : NX * (b + 1), :LANES] for b in range(BLOCKS)]
    imag = [out[NX * b : NX * (b + 1), LANES:] for b in range(BLOCKS)]
    return real, imag


def x_product(cols, tab):
    high, low = halves(cols)
    return mul(tab, jnp.concatenate([high, high, low], axis=0))


def pair_potential(rho_r, rho_i, kernel, yz_tab, x_tab, tw_r, tw_i):
    real, imag = butterflies(rho_r, rho_i, -1)
    turned_r = [real[c] * tw_r[c] - imag[c] * tw_i[c] for c in range(BLOCKS)]
    turned_i = [real[c] * tw_i[c] + imag[c] * tw_r[c] for c in range(BLOCKS)]
    real, imag = yz_product(turned_r, turned_i, yz_tab[0], yz_tab[1])
    cols = jnp.concatenate(
        [jnp.concatenate([real[c], imag[c]], axis=0) for c in range(BLOCKS)], axis=1
    )
    spectrum = x_product(cols, x_tab[0])
    weight = jnp.concatenate(kernel, axis=1)
    spectrum = spectrum * jnp.concatenate([weight, weight], axis=0)
    cols = x_product(spectrum, x_tab[1])
    real = [cols[:NX, LANES * c : LANES * (c + 1)] for c in range(BLOCKS)]
    imag = [cols[NX:, LANES * c : LANES * (c + 1)] for c in range(BLOCKS)]
    real, imag = yz_product(real, imag, yz_tab[2], yz_tab[3])
    turned_r = [real[c] * tw_r[c] + imag[c] * tw_i[c] for c in range(BLOCKS)]
    turned_i = [imag[c] * tw_r[c] - real[c] * tw_i[c] for c in range(BLOCKS)]
    return butterflies(turned_r, turned_i, 1)


def signed(index, length):
    return jnp.where(index >= length // 2, index - length, index).astype(jnp.float32)


def screened(block, qx, qy, qz):
    shape = (NX, LANES)
    lane = lax.broadcasted_iota(jnp.int32, shape, 1)
    gx = signed(lax.broadcasted_iota(jnp.int32, shape, 0), NX) * GSCALE + qx
    gy = signed(block + 8 * (lane // NZ), NY) * GSCALE + qy
    gz = signed(lane % NZ, NZ) * GSCALE + qz
    squares = gx * gx + gy * gy + gz * gz
    return (4.0 * math.pi * -0.5 / (NX * NY * NZ)) / (squares + SCREEN)


def reordered(keep, block, roll):
    group = lax.broadcasted_iota(jnp.int32, (NX, LANES), 1) // NZ
    out = None
    for d in range(4):
        source, place = 2 * d + block // 4, block % 4
        piece = roll(keep(source), ((d - place) * NZ) % LANES)
        out = piece if out is None else jnp.where(group == d, piece, out)
    return out


def kernel(
    tgt_in, occ_in, qvectors_in, qmap_in, cut_in, yz_in, x_in, twiddle_in,
    out_ref,
    qvectors, qmap, yz_tab, x_tab, twiddle, tgt, occ, cut, weight, part, other, summed, near, own, mid, total, gathered,
    entered, local_sem, occ_recv, in_send, in_recv, near_send, near_recv, mid_send, mid_recv, back_send, back_recv,
):
    k = lax.axis_index("ka")
    z = lax.axis_index("band")
    core = lax.axis_index("grid")
    far_core = 1 - core
    points = lax.axis_size("ka")
    chips = lax.axis_size("band")

    def chip(delta):
        return lax.rem(z + delta + chips, chips)

    def remote(src, dst, send, recv, where):
        return pltpu.make_async_remote_copy(
            src_ref=src, dst_ref=dst, send_sem=send, recv_sem=recv, device_id=where, device_id_type=MESH
        )

    locals_ = [
        pltpu.make_async_copy(tgt_in.at[0, 0], tgt.at[core], local_sem.at[0]),
        pltpu.make_async_copy(cut_in, cut.at[core], local_sem.at[1]),
        pltpu.make_async_copy(yz_in, yz_tab, local_sem.at[3]),
        pltpu.make_async_copy(x_in, x_tab, local_sem.at[4]),
        pltpu.make_async_copy(twiddle_in, twiddle, local_sem.at[5]),
        pltpu.make_async_copy(qvectors_in, qvectors, local_sem.at[6]),
        pltpu.make_async_copy(qmap_in, qmap, local_sem.at[7]),
    ]
    barrier = pltpu.get_barrier_semaphore()
    pl.semaphore_signal(barrier, inc=1, device_id={"grid": far_core}, device_id_type=MESH)

    @pl.when(core == 1)
    def _():
        source = lax.rem(k + HOP, points)
        for c in range(2):
            pl.semaphore_signal(barrier, inc=1, device_id={"ka": source, "grid": c}, device_id_type=MESH)

    for delta in NEAR:
        pl.semaphore_signal(barrier, inc=1, device_id={"band": chip(delta)}, device_id_type=MESH)

    for copy in locals_:
        copy.start()
    own_occ = pltpu.make_async_copy(occ_in.at[0, 0], occ.at[0], local_sem.at[2])

    @pl.when(core == 0)
    def _():
        own_occ.start()

    pl.semaphore_wait(barrier, 2 + len(NEAR))

    def tell(stage):
        for delta in (4, -4):
            pl.semaphore_signal(entered.at[stage], inc=1, device_id={"band": chip(delta)}, device_id_type=MESH)

    def hear(stage):
        pl.semaphore_wait(entered.at[stage], 2)

    user = lax.rem(k - HOP + points, points)
    sent = [
        remote(occ_in.at[0, 0], occ.at[core], in_send.at[0], occ_recv.at[core], {"ka": user, "grid": 1}),
        remote(tgt_in.at[0, 0], tgt.at[core], in_send.at[1], in_recv.at[1], {"grid": far_core}),
        remote(cut_in, cut.at[core], in_send.at[2], in_recv.at[2], {"grid": far_core}),
    ]
    for copy in sent:
        copy.start()
    cross = remote(occ_in.at[0, 0], occ.at[1], in_send.at[3], occ_recv.at[1], {"grid": 0})

    @pl.when(core == 1)
    def _():
        cross.start()

    tell(0)
    for n in (5, 6):
        locals_[n].wait()
    chosen = qmap[k]
    used = core.astype(jnp.float32)
    qx, qy, qz = (qvectors[d, chosen] * used for d in range(3))
    for block in range(BLOCKS):
        weight[block] = screened(block, qx, qy, qz)

    locals_[1].wait()
    sent[2].wait_recv()

    def keep(block):
        lanes = slice(LANES * block, LANES * (block + 1))
        return jnp.concatenate([cut[0, :, lanes], cut[1, :, lanes]], axis=0).astype(jnp.float32)

    for block in range(BLOCKS):
        weight[block] = weight[block] * reordered(keep, block, lambda v, s: pltpu.roll(v, s, 1))

    for n in (0, 2, 3, 4):
        locals_[n].wait()
    sent[1].wait_recv()
    hear(0)
    tell(1)

    @pl.when(core == 0)
    def _():
        own_occ.wait()
        cross.wait_recv()

    @pl.when(core == 1)
    def _():
        for c in range(2):
            remote(occ_in.at[0, 0], occ.at[c], in_send.at[0], occ_recv.at[c], {"grid": 0}).wait_recv()

    def block_of(ref, which, block):
        lanes = slice(LANES * block, LANES * (block + 1))
        return jnp.concatenate([ref[0, which, :, lanes], ref[1, which, :, lanes]], axis=0)

    rho_r, rho_i = [], []
    for block in range(BLOCKS):
        t_r, t_i = block_of(tgt, 0, block), block_of(tgt, 1, block)
        o_r, o_i = block_of(occ, 0, block), block_of(occ, 1, block)
        rho_r.append(o_r * t_r + o_i * t_i)
        rho_i.append(o_r * t_i - o_i * t_r)
    pot_r, pot_i = pair_potential(
        rho_r,
        rho_i,
        [weight[block] for block in range(BLOCKS)],
        [yz_tab[i] for i in range(4)],
        [x_tab[i] for i in range(2)],
        [twiddle[c : c + 1, :] for c in range(BLOCKS)],
        [twiddle[BLOCKS + c : BLOCKS + c + 1, :] for c in range(BLOCKS)],
    )
    for block in range(BLOCKS):
        o_r, o_i = block_of(occ, 0, block), block_of(occ, 1, block)
        app_r = o_r * pot_r[block] - o_i * pot_i[block]
        app_i = o_r * pot_i[block] + o_i * pot_r[block]
        for half in range(2):
            rows = slice(HALF * half, HALF * (half + 1))
            part[half, block, 0] = app_r[rows]
            part[half, block, 1] = app_i[rows]

    crossing = remote(part.at[far_core], other, in_send.at[4], in_recv.at[4], {"grid": far_core})
    crossing.start()
    crossing.wait_recv()
    summed[...] = part[core] + other[...]

    group = lax.rem(z, GROUPS)

    def pieces(ref, index, delta):
        if abs(delta) < 4:
            return ref.at[index]
        return ref.at[index, 0 if delta > 0 else 1]

    copies = []
    for n, delta in enumerate(NEAR):
        theirs = lax.rem(z + delta + GROUPS, GROUPS)
        slot = 0 if abs(delta) == 4 else n - 1
        copies.append(
            remote(
                pieces(summed, theirs, delta),
                pieces(near, slot, delta),
                near_send.at[n],
                near_recv.at[n],
                {"band": chip(delta)},
            )
        )
        copies[-1].start()
    value = summed[group]
    for copy in copies[::-1]:
        copy.wait_recv()
    for slot in range(len(NEAR) - 1):
        value = value + near[slot]
    own[...] = value

    hear(1)
    across = [
        remote(own, mid.at[n], mid_send.at[n], mid_recv.at[n], {"band": chip(delta)})
        for n, delta in enumerate((12, -12, 4, -4))
    ]
    for copy in across:
        copy.start()
    for copy in across[::-1]:
        copy.wait_recv()
    value = (mid[0] + mid[3]) + (mid[1] + mid[2])
    group = lax.rem(z + 4, GROUPS)
    total[...] = value
    gathered[group] = value

    back = []
    for n, delta in enumerate(NEAR):
        source = total if abs(delta) < 4 else total.at[0 if delta > 0 else 1]
        back.append(
            remote(
                source, pieces(gathered, group, delta), back_send.at[n], back_recv.at[n], {"band": chip(delta)}
            )
        )
        back[-1].start()
    for copy in back[::-1]:
        copy.wait_recv()
    for block in range(BLOCKS):
        lanes = slice(LANES * block, LANES * (block + 1))
        for which in range(2):
            out_ref[0, 0, which, :, lanes] = gathered[block, which]

    for copy in [*sent, crossing, *copies, *across, *back]:
        copy.wait_send()

    @pl.when(core == 1)
    def _():
        cross.wait_send()


def shards(target_bands, occupied, qvectors, qmap, cutoff):
    yz_tab, x_tab, twiddle = make_tables()
    f32 = jnp.float32
    planes = (2, HALF, NY * NZ)
    tile = (2, HALF, LANES)
    dma = pltpu.SemaphoreType.DMA
    vmem = pl.BlockSpec(memory_space=pltpu.VMEM)
    anywhere = pl.BlockSpec(memory_space=pl.ANY)
    return pl.pallas_call(
        kernel,
        out_shape=pltpu.VMEM(target_bands.shape, f32),
        in_specs=[anywhere] * 8,
        out_specs=vmem,
        scratch_shapes=[
            pltpu.SMEM(qvectors.shape[::-1], f32),
            pltpu.SMEM(qmap.shape, jnp.int32),
            pltpu.VMEM(yz_tab.shape, jnp.bfloat16),
            pltpu.VMEM(x_tab.shape, jnp.bfloat16),
            pltpu.VMEM(twiddle.shape, f32),
            pltpu.VMEM((2,) + planes, f32),
            pltpu.VMEM((2,) + planes, f32),
            pltpu.VMEM(planes, jnp.int32),
            pltpu.VMEM((BLOCKS, NX, LANES), f32),
            pltpu.VMEM((2, BLOCKS) + tile, f32),
            pltpu.VMEM((BLOCKS,) + tile, f32),
            pltpu.VMEM((BLOCKS,) + tile, f32),
            pltpu.VMEM((len(NEAR) - 1,) + tile, f32),
            pltpu.VMEM(tile, f32),
            pltpu.VMEM((4,) + tile, f32),
            pltpu.VMEM(tile, f32),
            pltpu.VMEM((GROUPS,) + tile, f32),
            pltpu.SemaphoreType.REGULAR((2,)),
            dma((8,)),
            dma((2,)),
            dma((5,)),
            dma((5,)),
            dma((len(NEAR),)),
            dma((len(NEAR),)),
            dma((4,)),
            dma((4,)),
            dma((len(NEAR),)),
            dma((len(NEAR),)),
        ],
        compiler_params=pltpu.CompilerParams(collective_id=0, has_side_effects=True, vmem_limit_bytes=24 * 2**20),
    )(
        *(
            pltpu.with_memory_space_constraint(value, pltpu.HBM)
            for value in (target_bands, occupied, qvectors.T, qmap, cutoff, *map(jnp.asarray, (yz_tab, x_tab, twiddle)))
        )
    )


def solution(mesh):
    return jax.shard_map(
        shards,
        mesh=mesh,
        in_specs=(
            P("ka", None, None, "grid", None),
            P("ka", "band", None, "grid", None),
            P(),
            P(),
            P("grid", None),
        ),
        out_specs=P("ka", None, None, "grid", None),
        check_vma=False,
    )
```

```python
import functools
import math

import jax
import jax.numpy as jnp
import ml_dtypes
import numpy as np
from jax import lax
from jax.experimental import pallas as pl
from jax.experimental.pallas import tpu as pltpu
from jax.sharding import PartitionSpec as P

NX = 32
NY = 32
NZ = 32
HOP = 1
SCREEN = 1.0
GSCALE = 0.5

LANES = 128
BLOCKS = NY * NZ // LANES
HALF = NX // 2
GROUPS = 8
NEAR = (4, -4, 3, -3, 2, -2, 1, -1)
MESH = pl.DeviceIdType.MESH


def split_bf16(table):
    table = table.astype(np.float32)
    high = table.astype(ml_dtypes.bfloat16)
    low = (table - high.astype(np.float32)).astype(ml_dtypes.bfloat16)
    return high, low


def make_tables():
    lane = np.arange(LANES)
    low_y, z = lane // NZ, lane % NZ
    phase = np.outer(low_y, low_y) / 4.0 + (np.outer(z, z) % NZ) / NZ
    cos, sin = np.cos(2 * np.pi * phase), np.sin(2 * np.pi * phase)
    forward = np.block([[cos, -sin], [sin, cos]])
    backward = np.block([[cos, sin], [-sin, cos]])
    yz = np.stack([*split_bf16(forward), *split_bf16(backward)])
    x = np.arange(NX)
    angle = 2 * np.pi * (np.outer(x, x) % NX) / NX
    cos, sin = np.cos(angle), np.sin(angle)
    rows = []
    for mat in (np.block([[cos, sin], [-sin, cos]]), np.block([[cos, -sin], [sin, cos]])):
        high, low = split_bf16(mat)
        rows.append(np.concatenate([high, low, high], axis=1))
    turn = 2 * np.pi * np.outer(np.arange(BLOCKS), low_y) / NY
    twiddle = np.concatenate([np.cos(turn), -np.sin(turn)]).astype(np.float32)
    return yz, np.stack(rows), twiddle


def butterflies(real, imag, sign):
    count = len(real)
    if count == 1:
        return real, imag
    even_r, even_i = butterflies(real[::2], imag[::2], sign)
    odd_r, odd_i = butterflies(real[1::2], imag[1::2], sign)
    half = count // 2
    root = math.sqrt(0.5)
    out_r, out_i = [None] * count, [None] * count
    for k in range(half):
        r, i = odd_r[k], odd_i[k]
        turn = k * 8 // count
        if turn == 1:
            r, i = ((r - i) * root, (i + r) * root) if sign > 0 else ((r + i) * root, (i - r) * root)
        elif turn == 2:
            r, i = (-i, r) if sign > 0 else (i, -r)
        elif turn == 3:
            r, i = ((-r - i) * root, (r - i) * root) if sign > 0 else ((i - r) * root, (-i - r) * root)
        out_r[k], out_i[k] = even_r[k] + r, even_i[k] + i
        out_r[k + half], out_i[k + half] = even_r[k] - r, even_i[k] - i
    return out_r, out_i


def halves(value):
    high = value.astype(jnp.bfloat16)
    return high, (value - high.astype(jnp.float32)).astype(jnp.bfloat16)


def mul(a, b):
    return jnp.dot(a, b, preferred_element_type=jnp.float32)


def yz_product(real, imag, high_tab, low_tab):
    rows = jnp.concatenate(
        [jnp.concatenate(real, axis=0), jnp.concatenate(imag, axis=0)], axis=1
    )
    high, low = halves(rows)
    out = mul(high, high_tab) + (mul(low, high_tab) + mul(high, low_tab))
    count = real[0].shape[0]
    real = [out[count * b : count * (b + 1), :LANES] for b in range(BLOCKS)]
    imag = [out[count * b : count * (b + 1), LANES:] for b in range(BLOCKS)]
    return real, imag


def x_product(cols, tab):
    high, low = halves(cols)
    return mul(tab, jnp.concatenate([high, high, low], axis=0))


def screened_spectrum(rho_r, rho_i, kernel, yz_tab, x_tab, tw_r, tw_i):
    real, imag = butterflies(rho_r, rho_i, -1)
    turned_r = [real[c] * tw_r[c] - imag[c] * tw_i[c] for c in range(BLOCKS)]
    turned_i = [real[c] * tw_i[c] + imag[c] * tw_r[c] for c in range(BLOCKS)]
    real, imag = yz_product(turned_r, turned_i, yz_tab[0], yz_tab[1])
    cols = jnp.concatenate(
        [jnp.concatenate([real[c], imag[c]], axis=0) for c in range(BLOCKS)], axis=1
    )
    spectrum = x_product(cols, x_tab[0])
    weight = jnp.concatenate(kernel, axis=1)
    spectrum = spectrum * jnp.concatenate([weight, weight], axis=0)
    cols = x_product(spectrum, x_tab[1])
    real = [cols[:NX, LANES * c : LANES * (c + 1)] for c in range(BLOCKS)]
    imag = [cols[NX:, LANES * c : LANES * (c + 1)] for c in range(BLOCKS)]
    return real, imag


def back_along_yz(real, imag, yz_tab, tw_r, tw_i):
    real, imag = yz_product(real, imag, yz_tab[2], yz_tab[3])
    turned_r = [real[c] * tw_r[c] + imag[c] * tw_i[c] for c in range(BLOCKS)]
    turned_i = [imag[c] * tw_r[c] - real[c] * tw_i[c] for c in range(BLOCKS)]
    return butterflies(turned_r, turned_i, 1)


def signed(index, length):
    return jnp.where(index >= length // 2, index - length, index).astype(jnp.float32)


def screened(block, qx, qy, qz):
    shape = (NX, LANES)
    lane = lax.broadcasted_iota(jnp.int32, shape, 1)
    gx = signed(lax.broadcasted_iota(jnp.int32, shape, 0), NX) * GSCALE + qx
    gy = signed(block + 8 * (lane // NZ), NY) * GSCALE + qy
    gz = signed(lane % NZ, NZ) * GSCALE + qz
    squares = gx * gx + gy * gy + gz * gz
    return (4.0 * math.pi * -0.5 / (NX * NY * NZ)) / (squares + SCREEN)


def reordered(keep, block, roll):
    group = lax.broadcasted_iota(jnp.int32, (NX, LANES), 1) // NZ
    out = None
    for d in range(4):
        source, place = 2 * d + block // 4, block % 4
        piece = roll(keep(source), ((d - place) * NZ) % LANES)
        out = piece if out is None else jnp.where(group == d, piece, out)
    return out


def kernel(
    tgt_in, occ_in, qvectors_in, qmap_in, cut_in, yz_in, x_in, twiddle_in,
    out_ref,
    qvectors, qmap, yz_tab, x_tab, twiddle, tgt, occ, cut, weight, part, other, summed, near, own, mid, total, gathered,
    entered, local_sem, occ_recv, in_send, in_recv, near_send, near_recv, mid_send, mid_recv, back_send, back_recv,
):
    k = lax.axis_index("ka")
    z = lax.axis_index("band")
    core = lax.axis_index("grid")
    far_core = 1 - core
    points = lax.axis_size("ka")
    chips = lax.axis_size("band")

    def chip(delta):
        return lax.rem(z + delta + chips, chips)

    def remote(src, dst, send, recv, where):
        return pltpu.make_async_remote_copy(
            src_ref=src, dst_ref=dst, send_sem=send, recv_sem=recv, device_id=where, device_id_type=MESH
        )

    locals_ = [
        pltpu.make_async_copy(tgt_in.at[0, 0], tgt.at[core], local_sem.at[0]),
        pltpu.make_async_copy(cut_in, cut.at[core], local_sem.at[1]),
        pltpu.make_async_copy(yz_in, yz_tab, local_sem.at[3]),
        pltpu.make_async_copy(x_in, x_tab, local_sem.at[4]),
        pltpu.make_async_copy(twiddle_in, twiddle, local_sem.at[5]),
        pltpu.make_async_copy(qvectors_in, qvectors, local_sem.at[6]),
        pltpu.make_async_copy(qmap_in, qmap, local_sem.at[7]),
    ]
    barrier = pltpu.get_barrier_semaphore()
    pl.semaphore_signal(barrier, inc=1, device_id={"grid": far_core}, device_id_type=MESH)

    @pl.when(core == 1)
    def _():
        source = lax.rem(k + HOP, points)
        for c in range(2):
            pl.semaphore_signal(barrier, inc=1, device_id={"ka": source, "grid": c}, device_id_type=MESH)

    for delta in NEAR:
        pl.semaphore_signal(barrier, inc=1, device_id={"band": chip(delta)}, device_id_type=MESH)

    for copy in locals_:
        copy.start()
    own_occ = pltpu.make_async_copy(occ_in.at[0, 0], occ.at[0], local_sem.at[2])

    @pl.when(core == 0)
    def _():
        own_occ.start()

    pl.semaphore_wait(barrier, 2 + len(NEAR))

    def tell(stage):
        for delta in (4, -4):
            pl.semaphore_signal(entered.at[stage], inc=1, device_id={"band": chip(delta)}, device_id_type=MESH)

    def hear(stage):
        pl.semaphore_wait(entered.at[stage], 2)

    user = lax.rem(k - HOP + points, points)
    sent = [
        remote(occ_in.at[0, 0], occ.at[core], in_send.at[0], occ_recv.at[core], {"ka": user, "grid": 1}),
        remote(tgt_in.at[0, 0], tgt.at[core], in_send.at[1], in_recv.at[1], {"grid": far_core}),
        remote(cut_in, cut.at[core], in_send.at[2], in_recv.at[2], {"grid": far_core}),
    ]
    tell(0)
    for copy in sent:
        copy.start()
    cross = remote(occ_in.at[0, 0], occ.at[1], in_send.at[3], occ_recv.at[1], {"grid": 0})

    @pl.when(core == 1)
    def _():
        cross.start()

    for n in (5, 6):
        locals_[n].wait()
    chosen = qmap[k]
    used = core.astype(jnp.float32)
    qx, qy, qz = (qvectors[d, chosen] * used for d in range(3))
    for block in range(BLOCKS):
        weight[block] = screened(block, qx, qy, qz)

    locals_[1].wait()
    sent[2].wait_recv()

    def keep(block):
        lanes = slice(LANES * block, LANES * (block + 1))
        return jnp.concatenate([cut[0, :, lanes], cut[1, :, lanes]], axis=0).astype(jnp.float32)

    for block in range(BLOCKS):
        weight[block] = weight[block] * reordered(keep, block, lambda v, s: pltpu.roll(v, s, 1))

    for n in (0, 2, 3, 4):
        locals_[n].wait()
    sent[1].wait_recv()
    hear(0)
    tell(1)

    @pl.when(core == 0)
    def _():
        own_occ.wait()
        cross.wait_recv()

    @pl.when(core == 1)
    def _():
        for c in range(2):
            remote(occ_in.at[0, 0], occ.at[c], in_send.at[0], occ_recv.at[c], {"grid": 0}).wait_recv()

    def block_of(ref, which, block):
        lanes = slice(LANES * block, LANES * (block + 1))
        return jnp.concatenate([ref[0, which, :, lanes], ref[1, which, :, lanes]], axis=0)

    rho_r, rho_i = [], []
    for block in range(BLOCKS):
        t_r, t_i = block_of(tgt, 0, block), block_of(tgt, 1, block)
        o_r, o_i = block_of(occ, 0, block), block_of(occ, 1, block)
        rho_r.append(o_r * t_r + o_i * t_i)
        rho_i.append(o_r * t_i - o_i * t_r)
    tables = [yz_tab[i] for i in range(4)]
    tw_r = [twiddle[c : c + 1, :] for c in range(BLOCKS)]
    tw_i = [twiddle[BLOCKS + c : BLOCKS + c + 1, :] for c in range(BLOCKS)]
    real, imag = screened_spectrum(
        rho_r,
        rho_i,
        [weight[block] for block in range(BLOCKS)],
        tables,
        [x_tab[i] for i in range(2)],
        tw_r,
        tw_i,
    )

    crossings = []
    for n in range(4):
        where = pl.ds(2 * n, 2)
        crossings.append(
            remote(part.at[far_core, where], other.at[where], in_send.at[4 + n], in_recv.at[4 + n], {"grid": far_core})
        )

    def send():
        for copy in crossings:
            copy.start()

    for half in range(2):
        rows = slice(HALF * half, HALF * (half + 1))
        pot_r, pot_i = back_along_yz([r[rows] for r in real], [i[rows] for i in imag], tables, tw_r, tw_i)
        for block in range(BLOCKS):
            lanes = slice(LANES * block, LANES * (block + 1))
            o_r, o_i = occ[half, 0, :, lanes], occ[half, 1, :, lanes]
            part[half, block, 0] = o_r * pot_r[block] - o_i * pot_i[block]
            part[half, block, 1] = o_r * pot_i[block] + o_i * pot_r[block]
        pl.when(core == 1 - half)(send)
    for n, copy in enumerate(crossings):
        copy.wait_recv()
        where = slice(2 * n, 2 * n + 2)
        summed[where] = part[core, where] + other[where]

    group = lax.rem(z, GROUPS)

    def pieces(ref, index, delta):
        if abs(delta) < 4:
            return ref.at[index]
        return ref.at[index, 0 if delta > 0 else 1]

    copies = []
    for n, delta in enumerate(NEAR):
        theirs = lax.rem(z + delta + GROUPS, GROUPS)
        slot = 0 if abs(delta) == 4 else n - 1
        copies.append(
            remote(
                pieces(summed, theirs, delta),
                pieces(near, slot, delta),
                near_send.at[n],
                near_recv.at[n],
                {"band": chip(delta)},
            )
        )
        copies[-1].start()
    value = summed[group]
    for copy in copies[::-1]:
        copy.wait_recv()
    for slot in range(len(NEAR) - 1):
        value = value + near[slot]
    own[...] = value

    hear(1)
    across = [
        remote(own, mid.at[n], mid_send.at[n], mid_recv.at[n], {"band": chip(delta)})
        for n, delta in enumerate((12, -12, 4, -4))
    ]
    for copy in across:
        copy.start()
    for copy in across[::-1]:
        copy.wait_recv()
    value = (mid[0] + mid[3]) + (mid[1] + mid[2])
    group = lax.rem(z + 4, GROUPS)
    total[...] = value
    gathered[group] = value

    back = []
    for n, delta in enumerate(NEAR):
        source = total if abs(delta) < 4 else total.at[0 if delta > 0 else 1]
        back.append(
            remote(
                source, pieces(gathered, group, delta), back_send.at[n], back_recv.at[n], {"band": chip(delta)}
            )
        )
        back[-1].start()
    for copy in back[::-1]:
        copy.wait_recv()
    for block in range(BLOCKS):
        lanes = slice(LANES * block, LANES * (block + 1))
        for which in range(2):
            out_ref[0, 0, which, :, lanes] = gathered[block, which]

    for copy in [*sent, *crossings, *copies, *across, *back]:
        copy.wait_send()

    @pl.when(core == 1)
    def _():
        cross.wait_send()


def shards(target_bands, occupied, qvectors, qmap, cutoff):
    yz_tab, x_tab, twiddle = make_tables()
    f32 = jnp.float32
    planes = (2, HALF, NY * NZ)
    tile = (2, HALF, LANES)
    dma = pltpu.SemaphoreType.DMA
    vmem = pl.BlockSpec(memory_space=pltpu.VMEM)
    anywhere = pl.BlockSpec(memory_space=pl.ANY)
    return pl.pallas_call(
        kernel,
        out_shape=pltpu.VMEM(target_bands.shape, f32),
        in_specs=[anywhere] * 8,
        out_specs=vmem,
        scratch_shapes=[
            pltpu.SMEM(qvectors.shape[::-1], f32),
            pltpu.SMEM(qmap.shape, jnp.int32),
            pltpu.VMEM(yz_tab.shape, jnp.bfloat16),
            pltpu.VMEM(x_tab.shape, jnp.bfloat16),
            pltpu.VMEM(twiddle.shape, f32),
            pltpu.VMEM((2,) + planes, f32),
            pltpu.VMEM((2,) + planes, f32),
            pltpu.VMEM(planes, jnp.int32),
            pltpu.VMEM((BLOCKS, NX, LANES), f32),
            pltpu.VMEM((2, BLOCKS) + tile, f32),
            pltpu.VMEM((BLOCKS,) + tile, f32),
            pltpu.VMEM((BLOCKS,) + tile, f32),
            pltpu.VMEM((len(NEAR) - 1,) + tile, f32),
            pltpu.VMEM(tile, f32),
            pltpu.VMEM((4,) + tile, f32),
            pltpu.VMEM(tile, f32),
            pltpu.VMEM((GROUPS,) + tile, f32),
            pltpu.SemaphoreType.REGULAR((2,)),
            dma((8,)),
            dma((2,)),
            dma((8,)),
            dma((8,)),
            dma((len(NEAR),)),
            dma((len(NEAR),)),
            dma((4,)),
            dma((4,)),
            dma((len(NEAR),)),
            dma((len(NEAR),)),
        ],
        compiler_params=pltpu.CompilerParams(collective_id=0, has_side_effects=True, vmem_limit_bytes=24 * 2**20),
    )(
        *(
            pltpu.with_memory_space_constraint(value, pltpu.HBM)
            for value in (target_bands, occupied, qvectors.T, qmap, cutoff, *map(jnp.asarray, (yz_tab, x_tab, twiddle)))
        )
    )


def solution(mesh):
    return jax.shard_map(
        shards,
        mesh=mesh,
        in_specs=(
            P("ka", None, None, "grid", None),
            P("ka", "band", None, "grid", None),
            P(),
            P(),
            P("grid", None),
        ),
        out_specs=P("ka", None, None, "grid", None),
        check_vma=False,
    )
```

```python
import functools
import math

import jax
import jax.numpy as jnp
import ml_dtypes
import numpy as np
from jax import lax
from jax.experimental import pallas as pl
from jax.experimental.pallas import tpu as pltpu
from jax.sharding import PartitionSpec as P

NX = 32
NY = 32
NZ = 32
HOP = 1
SCREEN = 1.0
GSCALE = 0.5

LANES = 128
BLOCKS = NY * NZ // LANES
HALF = NX // 2
GROUPS = 8
NEAR = (4, -4, 3, -3, 2, -2, 1, -1)
MESH = pl.DeviceIdType.MESH


def split_bf16(table):
    table = table.astype(np.float32)
    high = table.astype(ml_dtypes.bfloat16)
    low = (table - high.astype(np.float32)).astype(ml_dtypes.bfloat16)
    return high, low


def make_tables():
    lane = np.arange(LANES)
    low_y, z = lane // NZ, lane % NZ
    phase = np.outer(low_y, low_y) / 4.0 + (np.outer(z, z) % NZ) / NZ
    cos, sin = np.cos(2 * np.pi * phase), np.sin(2 * np.pi * phase)
    forward = np.block([[cos, -sin], [sin, cos]])
    backward = np.block([[cos, sin], [-sin, cos]])
    yz = np.stack([*split_bf16(forward), *split_bf16(backward)])
    x = np.arange(NX)
    angle = 2 * np.pi * (np.outer(x, x) % NX) / NX
    cos, sin = np.cos(angle), np.sin(angle)
    rows = []
    for mat in (np.block([[cos, sin], [-sin, cos]]), np.block([[cos, -sin], [sin, cos]])):
        high, low = split_bf16(mat)
        rows.append(np.concatenate([high, low, high], axis=1))
    turn = 2 * np.pi * np.outer(np.arange(BLOCKS), low_y) / NY
    twiddle = np.concatenate([np.cos(turn), -np.sin(turn)]).astype(np.float32)
    return yz, np.stack(rows), twiddle


def butterflies(real, imag, sign):
    count = len(real)
    if count == 1:
        return real, imag
    even_r, even_i = butterflies(real[::2], imag[::2], sign)
    odd_r, odd_i = butterflies(real[1::2], imag[1::2], sign)
    half = count // 2
    root = math.sqrt(0.5)
    out_r, out_i = [None] * count, [None] * count
    for k in range(half):
        r, i = odd_r[k], odd_i[k]
        turn = k * 8 // count
        if turn == 1:
            r, i = ((r - i) * root, (i + r) * root) if sign > 0 else ((r + i) * root, (i - r) * root)
        elif turn == 2:
            r, i = (-i, r) if sign > 0 else (i, -r)
        elif turn == 3:
            r, i = ((-r - i) * root, (r - i) * root) if sign > 0 else ((i - r) * root, (-i - r) * root)
        out_r[k], out_i[k] = even_r[k] + r, even_i[k] + i
        out_r[k + half], out_i[k + half] = even_r[k] - r, even_i[k] - i
    return out_r, out_i


def halves(value):
    high = value.astype(jnp.bfloat16)
    return high, (value - high.astype(jnp.float32)).astype(jnp.bfloat16)


def mul(a, b):
    return jnp.dot(a, b, preferred_element_type=jnp.float32)


def yz_product(real, imag, high_tab, low_tab):
    rows = jnp.concatenate(
        [jnp.concatenate(real, axis=0), jnp.concatenate(imag, axis=0)], axis=1
    )
    high, low = halves(rows)
    out = mul(high, high_tab) + (mul(low, high_tab) + mul(high, low_tab))
    real = [out[NX * b : NX * (b + 1), :LANES] for b in range(BLOCKS)]
    imag = [out[NX * b : NX * (b + 1), LANES:] for b in range(BLOCKS)]
    return real, imag


def x_product(cols, tab):
    high, low = halves(cols)
    return mul(tab, jnp.concatenate([high, high, low], axis=0))


def pair_potential(rho_r, rho_i, kernel, yz_tab, x_tab, tw_r, tw_i):
    real, imag = butterflies(rho_r, rho_i, -1)
    turned_r = [real[c] * tw_r[c] - imag[c] * tw_i[c] for c in range(BLOCKS)]
    turned_i = [real[c] * tw_i[c] + imag[c] * tw_r[c] for c in range(BLOCKS)]
    real, imag = yz_product(turned_r, turned_i, yz_tab[0], yz_tab[1])
    cols = jnp.concatenate(
        [jnp.concatenate([real[c], imag[c]], axis=0) for c in range(BLOCKS)], axis=1
    )
    spectrum = x_product(cols, x_tab[0])
    weight = jnp.concatenate(kernel, axis=1)
    spectrum = spectrum * jnp.concatenate([weight, weight], axis=0)
    cols = x_product(spectrum, x_tab[1])
    real = [cols[:NX, LANES * c : LANES * (c + 1)] for c in range(BLOCKS)]
    imag = [cols[NX:, LANES * c : LANES * (c + 1)] for c in range(BLOCKS)]
    real, imag = yz_product(real, imag, yz_tab[2], yz_tab[3])
    turned_r = [real[c] * tw_r[c] + imag[c] * tw_i[c] for c in range(BLOCKS)]
    turned_i = [imag[c] * tw_r[c] - real[c] * tw_i[c] for c in range(BLOCKS)]
    return butterflies(turned_r, turned_i, 1)


def signed(index, length):
    return jnp.where(index >= length // 2, index - length, index).astype(jnp.float32)


def screened(block, qx, qy, qz):
    shape = (NX, LANES)
    lane = lax.broadcasted_iota(jnp.int32, shape, 1)
    gx = signed(lax.broadcasted_iota(jnp.int32, shape, 0), NX) * GSCALE + qx
    gy = signed(block + 8 * (lane // NZ), NY) * GSCALE + qy
    gz = signed(lane % NZ, NZ) * GSCALE + qz
    squares = gx * gx + gy * gy + gz * gz
    return (4.0 * math.pi * -0.5 / (NX * NY * NZ)) / (squares + SCREEN)


def reordered(keep, block, roll):
    group = lax.broadcasted_iota(jnp.int32, (NX, LANES), 1) // NZ
    out = None
    for d in range(4):
        source, place = 2 * d + block // 4, block % 4
        piece = roll(keep(source), ((d - place) * NZ) % LANES)
        out = piece if out is None else jnp.where(group == d, piece, out)
    return out


def kernel(
    tgt_in, occ_in, qvectors_in, qmap_in, cut_in, yz_in, x_in, twiddle_in,
    out_ref,
    qvectors, qmap, yz_tab, x_tab, twiddle, tgt, occ, cut, weight, part, other, summed, near, own, mid, total, gathered,
    entered, local_sem, occ_recv, in_send, in_recv, near_send, near_recv, mid_send, mid_recv, back_send, back_recv,
):
    k = lax.axis_index("ka")
    z = lax.axis_index("band")
    core = lax.axis_index("grid")
    far_core = 1 - core
    points = lax.axis_size("ka")
    chips = lax.axis_size("band")

    def chip(delta):
        return lax.rem(z + delta + chips, chips)

    def remote(src, dst, send, recv, where):
        return pltpu.make_async_remote_copy(
            src_ref=src, dst_ref=dst, send_sem=send, recv_sem=recv, device_id=where, device_id_type=MESH
        )

    locals_ = [
        pltpu.make_async_copy(tgt_in.at[0, 0], tgt.at[core], local_sem.at[0]),
        pltpu.make_async_copy(cut_in, cut.at[core], local_sem.at[1]),
        pltpu.make_async_copy(yz_in, yz_tab, local_sem.at[3]),
        pltpu.make_async_copy(x_in, x_tab, local_sem.at[4]),
        pltpu.make_async_copy(twiddle_in, twiddle, local_sem.at[5]),
        pltpu.make_async_copy(qvectors_in, qvectors, local_sem.at[6]),
        pltpu.make_async_copy(qmap_in, qmap, local_sem.at[7]),
    ]
    barrier = pltpu.get_barrier_semaphore()
    pl.semaphore_signal(barrier, inc=1, device_id={"grid": far_core}, device_id_type=MESH)

    @pl.when(core == 1)
    def _():
        source = lax.rem(k + HOP, points)
        for c in range(2):
            pl.semaphore_signal(barrier, inc=1, device_id={"ka": source, "grid": c}, device_id_type=MESH)

    for delta in NEAR:
        pl.semaphore_signal(barrier, inc=1, device_id={"band": chip(delta)}, device_id_type=MESH)

    for copy in locals_:
        copy.start()
    own_occ = pltpu.make_async_copy(occ_in.at[0, 0], occ.at[0], local_sem.at[2])

    @pl.when(core == 0)
    def _():
        own_occ.start()

    pl.semaphore_wait(barrier, 2 + len(NEAR))

    def tell(stage):
        for delta in (4, -4):
            pl.semaphore_signal(entered.at[stage], inc=1, device_id={"band": chip(delta)}, device_id_type=MESH)

    def hear(stage):
        pl.semaphore_wait(entered.at[stage], 2)

    user = lax.rem(k - HOP + points, points)
    sent = [
        remote(occ_in.at[0, 0], occ.at[core], in_send.at[0], occ_recv.at[core], {"ka": user, "grid": 1}),
        remote(tgt_in.at[0, 0], tgt.at[core], in_send.at[1], in_recv.at[1], {"grid": far_core}),
        remote(cut_in, cut.at[core], in_send.at[2], in_recv.at[2], {"grid": far_core}),
    ]
    for copy in sent:
        copy.start()
    cross = remote(occ_in.at[0, 0], occ.at[1], in_send.at[3], occ_recv.at[1], {"grid": 0})

    @pl.when(core == 1)
    def _():
        cross.start()

    tell(0)
    for n in (5, 6):
        locals_[n].wait()
    chosen = qmap[k]
    used = core.astype(jnp.float32)
    qx, qy, qz = (qvectors[d, chosen] * used for d in range(3))
    for block in range(BLOCKS):
        weight[block] = screened(block, qx, qy, qz)

    locals_[1].wait()
    sent[2].wait_recv()

    def keep(block):
        lanes = slice(LANES * block, LANES * (block + 1))
        return jnp.concatenate([cut[0, :, lanes], cut[1, :, lanes]], axis=0).astype(jnp.float32)

    for block in range(BLOCKS):
        weight[block] = weight[block] * reordered(keep, block, lambda v, s: pltpu.roll(v, s, 1))

    for n in (0, 2, 3, 4):
        locals_[n].wait()
    sent[1].wait_recv()
    hear(0)
    tell(1)

    @pl.when(core == 0)
    def _():
        own_occ.wait()
        cross.wait_recv()

    @pl.when(core == 1)
    def _():
        for c in range(2):
            remote(occ_in.at[0, 0], occ.at[c], in_send.at[0], occ_recv.at[c], {"grid": 0}).wait_recv()

    def block_of(ref, which, block):
        lanes = slice(LANES * block, LANES * (block + 1))
        return jnp.concatenate([ref[0, which, :, lanes], ref[1, which, :, lanes]], axis=0)

    rho_r, rho_i = [], []
    for block in range(BLOCKS):
        t_r, t_i = block_of(tgt, 0, block), block_of(tgt, 1, block)
        o_r, o_i = block_of(occ, 0, block), block_of(occ, 1, block)
        rho_r.append(o_r * t_r + o_i * t_i)
        rho_i.append(o_r * t_i - o_i * t_r)
    pot_r, pot_i = pair_potential(
        rho_r,
        rho_i,
        [weight[block] for block in range(BLOCKS)],
        [yz_tab[i] for i in range(4)],
        [x_tab[i] for i in range(2)],
        [twiddle[c : c + 1, :] for c in range(BLOCKS)],
        [twiddle[BLOCKS + c : BLOCKS + c + 1, :] for c in range(BLOCKS)],
    )
    for block in range(BLOCKS):
        o_r, o_i = block_of(occ, 0, block), block_of(occ, 1, block)
        app_r = o_r * pot_r[block] - o_i * pot_i[block]
        app_i = o_r * pot_i[block] + o_i * pot_r[block]
        for half in range(2):
            rows = slice(HALF * half, HALF * (half + 1))
            part[half, block, 0] = app_r[rows]
            part[half, block, 1] = app_i[rows]

    crossing = remote(part.at[far_core], other, in_send.at[4], in_recv.at[4], {"grid": far_core})
    crossing.start()
    crossing.wait_recv()
    summed[...] = part[core] + other[...]

    group = lax.rem(z, GROUPS)

    def pieces(ref, index, delta):
        if abs(delta) < 4:
            return ref.at[index]
        return ref.at[index, 0 if delta > 0 else 1]

    copies = []
    for n, delta in enumerate(NEAR):
        theirs = lax.rem(z + delta + GROUPS, GROUPS)
        slot = 0 if abs(delta) == 4 else n - 1
        copies.append(
            remote(
                pieces(summed, theirs, delta),
                pieces(near, slot, delta),
                near_send.at[n],
                near_recv.at[n],
                {"band": chip(delta)},
            )
        )
        copies[-1].start()
    value = summed[group]
    for n in range(len(NEAR) - 1, 1, -1):
        copies[n].wait_recv()
        value = value + near[n - 1]
    for copy in copies[:2]:
        copy.wait_recv()
    value = value + near[0]
    own[...] = value

    hear(1)
    across = [
        remote(own, mid.at[n], mid_send.at[n], mid_recv.at[n], {"band": chip(delta)})
        for n, delta in enumerate((12, -12, 4, -4))
    ]
    for copy in across:
        copy.start()
    for copy in across[::-1]:
        copy.wait_recv()
    value = (mid[0] + mid[3]) + (mid[1] + mid[2])
    group = lax.rem(z + 4, GROUPS)
    total[...] = value
    gathered[group] = value

    back = []
    for n, delta in enumerate(NEAR):
        source = total if abs(delta) < 4 else total.at[0 if delta > 0 else 1]
        back.append(
            remote(
                source, pieces(gathered, group, delta), back_send.at[n], back_recv.at[n], {"band": chip(delta)}
            )
        )
        back[-1].start()
    def put(index):
        lanes = pl.ds(pl.multiple_of(index * LANES, LANES), LANES)
        for which in range(2):
            out_ref[0, 0, which, :, lanes] = gathered[index, which]

    put(group)
    for n in range(len(NEAR) - 1, 1, -1):
        back[n].wait_recv()
        put(lax.rem(group - NEAR[n] + GROUPS, GROUPS))
    for copy in back[:2]:
        copy.wait_recv()
    put(lax.rem(group + 4, GROUPS))

    for copy in [*sent, crossing, *copies, *across, *back]:
        copy.wait_send()

    @pl.when(core == 1)
    def _():
        cross.wait_send()


def shards(target_bands, occupied, qvectors, qmap, cutoff):
    yz_tab, x_tab, twiddle = make_tables()
    f32 = jnp.float32
    planes = (2, HALF, NY * NZ)
    tile = (2, HALF, LANES)
    dma = pltpu.SemaphoreType.DMA
    vmem = pl.BlockSpec(memory_space=pltpu.VMEM)
    anywhere = pl.BlockSpec(memory_space=pl.ANY)
    return pl.pallas_call(
        kernel,
        out_shape=pltpu.VMEM(target_bands.shape, f32),
        in_specs=[anywhere] * 8,
        out_specs=vmem,
        scratch_shapes=[
            pltpu.SMEM(qvectors.shape[::-1], f32),
            pltpu.SMEM(qmap.shape, jnp.int32),
            pltpu.VMEM(yz_tab.shape, jnp.bfloat16),
            pltpu.VMEM(x_tab.shape, jnp.bfloat16),
            pltpu.VMEM(twiddle.shape, f32),
            pltpu.VMEM((2,) + planes, f32),
            pltpu.VMEM((2,) + planes, f32),
            pltpu.VMEM(planes, jnp.int32),
            pltpu.VMEM((BLOCKS, NX, LANES), f32),
            pltpu.VMEM((2, BLOCKS) + tile, f32),
            pltpu.VMEM((BLOCKS,) + tile, f32),
            pltpu.VMEM((BLOCKS,) + tile, f32),
            pltpu.VMEM((len(NEAR) - 1,) + tile, f32),
            pltpu.VMEM(tile, f32),
            pltpu.VMEM((4,) + tile, f32),
            pltpu.VMEM(tile, f32),
            pltpu.VMEM((GROUPS,) + tile, f32),
            pltpu.SemaphoreType.REGULAR((2,)),
            dma((8,)),
            dma((2,)),
            dma((5,)),
            dma((5,)),
            dma((len(NEAR),)),
            dma((len(NEAR),)),
            dma((4,)),
            dma((4,)),
            dma((len(NEAR),)),
            dma((len(NEAR),)),
        ],
        compiler_params=pltpu.CompilerParams(collective_id=0, has_side_effects=True, vmem_limit_bytes=24 * 2**20),
    )(
        *(
            pltpu.with_memory_space_constraint(value, pltpu.HBM)
            for value in (target_bands, occupied, qvectors.T, qmap, cutoff, *map(jnp.asarray, (yz_tab, x_tab, twiddle)))
        )
    )


def solution(mesh):
    return jax.shard_map(
        shards,
        mesh=mesh,
        in_specs=(
            P("ka", None, None, "grid", None),
            P("ka", "band", None, "grid", None),
            P(),
            P(),
            P("grid", None),
        ),
        out_specs=P("ka", None, None, "grid", None),
        check_vma=False,
    )
```
